32 devices in a mesh: seq: 8 (over z, x), head: 4 (over y, core).
Axes of the slice: x: 2, y: 2, z: 4, core: 2. Of those that a mesh axis runs over, the one named last changes fastest.
Arguments:
- hidden_states: bfloat16 [2, 352, 5120], P(None, 'seq', 'head'), may hold values from -60 to 60
- clean_states: bfloat16 [2, 352, 5120], P(None, 'seq', 'head'), may hold values from -60 to 60
- w_query: bfloat16 [5120, 2560], P(None, 'head'), may hold values from -2 to 2
- w_key: bfloat16 [5120, 2560], P(None, 'head'), may hold values from -2 to 2
- w_value: bfloat16 [5120, 2560], P(None, 'head'), may hold values from -0.078125 to 0.078125
- q_gain: float32 [2560], P('head'), may hold values from 0.1 to 1.9
- k_gain: float32 [2560], P('head'), may hold values from 0.1 to 1.9
- cache_keys: bfloat16 [9, 352, 2560], P(None, 'seq', 'head'), may hold values from -1300 to 1300
- cache_values: bfloat16 [9, 352, 2560], P(None, 'seq', 'head'), may hold values from -6 to 6
- modulation: float32 [4, 2, 5120], replicated, may hold values from -3 to 3
- controls: int32 [3], replicated, may hold values from 0 to 6, as said below
- frame_pos: int32 [11], replicated, may hold values from 0 to 63
Outputs:
- attention_out: bfloat16 [2, 352, 2560], P(None, 'seq', 'head')
- new_keys: bfloat16 [9, 352, 2560], P(None, 'seq', 'head')
- new_values: bfloat16 [9, 352, 2560], P(None, 'seq', 'head')
The draws below stay inside these ranges and needn't reach their ends.
Inputs may be any that keep to these rules, and one draw needn't show every extreme that they name: controls[0] lies in 1 to 3, controls[1] in 0 to 6 and equal to 6 whenever controls[0] is below 3, controls[2] in 1 to 2.
All inputs are finite; a program needn't handle non-finite values.
Results may differ from the reference program's by a relative error of at most 0.011.
The reference program's roundings to bfloat16 on the way count: a program that leaves them out, or rounds other values in their place, can miss the bound.
Values may be sent and summed in bfloat16 or wider, within the bound.
A program may use at most 320 MiB of HBM per device.

```python
import math
import jax
import jax.numpy as jnp
from jax import lax

D = 5120
HEADS = 20
HD = 128
CACHE_FRAMES = 9
GROUP_FRAMES = 2
STEPS = 4
INNER = 2560
FRAME = 352


def feature_draw(key, salt):
    key = jax.random.fold_in(key, salt)
    first_key, second_key = jax.random.split(key, 2)
    scales = jnp.exp(jax.random.uniform(first_key, (D,), jnp.float32) * math.log(10.0))
    base = jax.random.normal(second_key, (GROUP_FRAMES, FRAME, D), jnp.float32)
    return jnp.clip(base * scales[None, None, :], -60.0, 60.0).astype(jnp.bfloat16)


def column_draw(key, salt):
    key = jax.random.fold_in(key, salt)
    first_key, second_key = jax.random.split(key, 2)
    ramp = jnp.arange(INNER, dtype=jnp.float32) / max(INNER - 1, 1)
    scales = jnp.exp(jax.random.uniform(first_key, (INNER,), jnp.float32) * math.log(10.0)) * jnp.power(3.0, 0.5 * ramp)
    base = jax.random.normal(second_key, (D, INNER), jnp.float32)
    return jnp.clip(base * scales[None, :] / (3.0 * math.sqrt(D)), -2.0, 2.0).astype(jnp.bfloat16)


def draw_hidden_states(key, part):
    return feature_draw(key, 101)


def draw_clean_states(key, part):
    return feature_draw(key, 202)


def draw_w_query(key, part):
    return column_draw(key, 303)


def draw_w_key(key, part):
    return column_draw(key, 404)


def draw_cache_keys(key, part):
    key = jax.random.fold_in(key, 505)
    first_key = jax.random.fold_in(key, 0)
    base = jnp.clip(jax.random.normal(first_key, (CACHE_FRAMES, FRAME, INNER), jnp.float32), -6.0, 6.0)
    return base.astype(jnp.bfloat16)


def draw_controls(key, part):
    key = jax.random.fold_in(key, 606)
    step_key, slot_key, sink_key = jax.random.split(key, 3)
    step_value = jax.random.randint(step_key, (1,), 1, STEPS, jnp.int32)
    free_slot = jax.random.randint(slot_key, (1,), 0, 7, jnp.int32)
    slot_value = jnp.where(step_value < STEPS - 1, jnp.int32(6), free_slot).astype(jnp.int32)
    sink_value = jax.random.randint(sink_key, (1,), 1, 3, jnp.int32)
    return jnp.concatenate([step_value, slot_value, sink_value], axis=0)


def touch_ends(array, stream_key, smallest, largest):
    shape = array.shape
    spot = [jax.random.randint(jax.random.fold_in(stream_key, axis), (), 0, shape[axis]) for axis in range(len(shape))]
    array = array.at[tuple(spot)].set(smallest)
    longest = shape.index(max(shape))
    spot[longest] = (spot[longest] + 1) % shape[longest]
    return array.at[tuple(spot)].set(largest)


def level_of(own_key, shape, cuts, smallest, high):
    def one(dim, blocks):
        steps = jax.random.uniform(jax.random.fold_in(jax.random.fold_in(own_key, 6), dim), (blocks,), jnp.float32, smallest / len(cuts), high / len(cuts))
        return jnp.repeat(jnp.exp(steps), shape[dim] // blocks).reshape((-1,) + (1,) * (len(shape) - dim - 1))

    loudness = one(*cuts[0])
    for cut in cuts[1:]:
        loudness = loudness * one(*cut)
    return loudness


def normal_values(stream_key, shape, scale, reach, cuts=(), kind=jnp.bfloat16):
    result = scale * jax.random.normal(stream_key, shape, jnp.float32)
    if cuts:
        result = result * level_of(stream_key, shape, cuts, -0.22, 0.18)
    return jnp.clip(result, -reach, reach).astype(kind)


def setup_inputs(seed: int = 0) -> dict:
    keys = jax.random.split(jax.random.key(seed), 13)
    return {
        "hidden_states": draw_hidden_states(jax.random.fold_in(keys[12], 71), 0),
        "clean_states": draw_clean_states(jax.random.fold_in(keys[12], 71), 0),
        "w_query": draw_w_query(jax.random.fold_in(keys[12], 71), 0),
        "w_key": draw_w_key(jax.random.fold_in(keys[12], 71), 0),
        "w_value": normal_values(keys[4], (D, INNER), D ** -0.5, 0.078125, ((1, 4),)),
        "q_gain": jnp.clip(1.0 + 0.18 * jax.random.normal(keys[5], (INNER,), jnp.float32), 0.1, 1.9),
        "k_gain": jnp.clip(1.0 + 0.18 * jax.random.normal(keys[6], (INNER,), jnp.float32), 0.1, 1.9),
        "cache_keys": draw_cache_keys(jax.random.fold_in(keys[12], 71), 0),
        "cache_values": normal_values(keys[8], (CACHE_FRAMES, FRAME, INNER), 1.0, 6.0, ((1, 8), (2, 4))),
        "modulation": normal_values(keys[9], (STEPS, 2, D), 0.5, 3.0, (), jnp.float32),
        "controls": draw_controls(jax.random.fold_in(keys[12], 71), 0),
        "frame_pos": touch_ends(jax.random.randint(keys[11], (CACHE_FRAMES + GROUP_FRAMES,), 0, 64), jax.random.fold_in(keys[11], 1), 0, 63).astype(jnp.int32),
    }


epsilon = 1e-06

def modulate(states, modulation, step_index):
    choose = (jnp.arange(modulation.shape[0], dtype=jnp.int32) == step_index).astype(jnp.float32)
    picked = lax.optimization_barrier(jnp.sum(choose[:, None, None] * modulation, axis=0))
    values = states.astype(jnp.float32)
    centre = lax.optimization_barrier(jnp.mean(values, axis=-1, keepdims=True))
    spread = lax.optimization_barrier(jnp.mean(jnp.square(values - centre), axis=-1, keepdims=True))
    normed = (values - centre) * lax.rsqrt(spread + epsilon)
    return (normed * (1.0 + picked[1]) + picked[0]).astype(jnp.bfloat16)

def rms_scale(values, square_total, width, gain):
    return values * lax.rsqrt(square_total / width + epsilon)[:, None] * gain

def rotate(values, time_pos, space_pos):
    head_size = values.shape[-1]
    half_size = head_size // 2
    time_pairs = (head_size - 4 * (head_size // 6)) // 2
    space_pairs = half_size - time_pairs
    pair_index = jnp.arange(half_size, dtype=jnp.int32)
    exponent = jnp.where(pair_index < time_pairs, pair_index / time_pairs, (pair_index - time_pairs) / space_pairs).astype(jnp.float32)
    frequency = jnp.power(10000.0, -exponent)
    is_time = (pair_index < time_pairs)[None, None, :]
    position = jnp.where(is_time, time_pos.astype(jnp.float32)[:, None, None], space_pos.astype(jnp.float32)[None, :, None])
    angle = position * frequency
    cosine = jnp.cos(angle)[:, :, None, :]
    sine = jnp.sin(angle)[:, :, None, :]
    first = values[..., :half_size]
    second = values[..., half_size:]
    return jnp.concatenate([first * cosine - second * sine, second * cosine + first * sine], axis=-1)

def write_cache(key_store, value_store, fresh_keys, fresh_values, slot_start, sinks):
    rolling = key_store.shape[0] - sinks
    for group_frame in range(fresh_keys.shape[0]):
        target = (sinks + (slot_start + group_frame) % rolling).astype(jnp.int32)
        anchor = (target, jnp.int32(0), jnp.int32(0))
        key_store = lax.dynamic_update_slice(key_store, fresh_keys[group_frame:group_frame + 1], anchor)
        value_store = lax.dynamic_update_slice(value_store, fresh_values[group_frame:group_frame + 1], anchor)
    return (key_store, value_store)

def one_head(operands):
    query_head, key_head, value_head = operands
    scores = jnp.dot(query_head, key_head.T, preferred_element_type=jnp.float32) * HD ** (-0.5)
    top_score = lax.optimization_barrier(jnp.max(scores, axis=-1))
    weights = jnp.exp(scores - top_score[:, None])
    totals = lax.optimization_barrier(jnp.sum(weights, axis=-1))
    summed = jnp.dot(weights.astype(jnp.bfloat16), value_head, preferred_element_type=jnp.float32)
    return (summed / totals[:, None]).astype(jnp.bfloat16)

def reference(hidden_states, clean_states, w_query, w_key, w_value, q_gain, k_gain, cache_keys, cache_values, modulation, controls, frame_pos):
    timestep = controls[0]
    write_slot = controls[1]
    sink_count = controls[2]
    all_rows = GROUP_FRAMES * FRAME
    noisy = modulate(hidden_states, modulation, timestep).reshape(all_rows, D)
    settled = modulate(clean_states, modulation, jnp.int32(0)).reshape(all_rows, D)
    query_raw = jnp.dot(noisy, w_query, preferred_element_type=jnp.float32)
    key_raw = jnp.dot(noisy, w_key, preferred_element_type=jnp.float32)
    key_clean = jnp.dot(settled, w_key, preferred_element_type=jnp.float32)
    value_new = jnp.dot(noisy, w_value, preferred_element_type=jnp.float32).astype(jnp.bfloat16)
    value_clean = jnp.dot(settled, w_value, preferred_element_type=jnp.float32).astype(jnp.bfloat16)
    query_norm = rms_scale(query_raw, lax.optimization_barrier(jnp.sum(query_raw * query_raw, axis=-1)), INNER, q_gain)
    key_norm = rms_scale(key_raw, lax.optimization_barrier(jnp.sum(key_raw * key_raw, axis=-1)), INNER, k_gain)
    stored_keys = rms_scale(key_clean, lax.optimization_barrier(jnp.sum(key_clean * key_clean, axis=-1)), INNER, k_gain).astype(jnp.bfloat16)
    space_pos = jnp.arange(FRAME, dtype=jnp.int32)
    group_time = frame_pos[CACHE_FRAMES:]
    cache_time = frame_pos[:CACHE_FRAMES]
    query_rot = rotate(query_norm.reshape(GROUP_FRAMES, FRAME, HEADS, HD), group_time, space_pos).astype(jnp.bfloat16)
    key_rot = rotate(key_norm.reshape(GROUP_FRAMES, FRAME, HEADS, HD), group_time, space_pos).astype(jnp.bfloat16)
    cache_rot = rotate(cache_keys.astype(jnp.float32).reshape(CACHE_FRAMES, FRAME, HEADS, HD), cache_time, space_pos).astype(jnp.bfloat16)
    keys_all = jnp.concatenate([cache_rot.reshape(-1, HEADS, HD), key_rot.reshape(-1, HEADS, HD)], axis=0)
    values_all = jnp.concatenate([cache_values.reshape(-1, HEADS, HD), value_new.reshape(-1, HEADS, HD)], axis=0)
    attended = lax.map(one_head, (jnp.transpose(query_rot.reshape(-1, HEADS, HD), (1, 0, 2)), jnp.transpose(keys_all, (1, 0, 2)), jnp.transpose(values_all, (1, 0, 2))))
    attention_out = jnp.transpose(attended, (1, 0, 2)).reshape(GROUP_FRAMES, FRAME, INNER)
    new_keys, new_values = write_cache(cache_keys, cache_values, stored_keys.reshape(GROUP_FRAMES, FRAME, INNER), value_clean.reshape(GROUP_FRAMES, FRAME, INNER), write_slot, sink_count)
    return (attention_out, new_keys, new_values)
```

```python
import contextlib
import functools

import jax
import jax.numpy as jnp
import numpy as np
from jax import lax
from jax.experimental import pallas as pl
from jax.experimental.pallas import tpu as pltpu
from jax.sharding import PartitionSpec as P

HD = 128
epsilon = 1e-06
GROUP = 4
CHUNKS = 2
F32 = jnp.float32
BF16 = jnp.bfloat16


def span(name):
    return contextlib.nullcontext()


def kernel(
    n_seq,
    n_head,
    x_noisy,
    x_clean,
    w_query,
    w_key,
    w_value,
    q_gain,
    k_gain,
    cache_keys,
    cache_values,
    modulation,
    frequency,
    controls,
    frame_pos,
    out_ref,
    fresh_keys,
    fresh_values,
    w_vmem,
    mod_vmem,
    keys_vmem,
    values_vmem,
    xg,
    y,
    acc,
    acc_b,
    flip,
    table,
    k32,
    v32,
    kst,
    vst,
    kx,
    vx,
    ks,
    vs,
    q_st,
    qx,
    qs,
    part_x,
    part_s,
    stat_st,
    px,
    ps,
    st,
    ss_send,
    ss_recv,
    w_sem,
    in_sem,
    x_in_sem,
    x_send_sem,
    x_fwd_sem,
    x_recv_sem,
    ss_send_sem,
    ss_recv_sem,
    kv_send_sem,
    kv_recv_sem,
    sh_send_sem,
    sh_recv_sem,
    qx_send_sem,
    qx_recv_sem,
    qs_send_sem,
    qs_recv_sem,
    px_send_sem,
    px_recv_sem,
    ps_send_sem,
    ps_recv_sem,
    st_send_sem,
    st_recv_sem,
):
    seq = lax.axis_index("seq")
    head = lax.axis_index("head")
    frame, groups, shard = x_noisy.shape
    rows = frame * groups
    blocks = shard // HD
    chunk = blocks // CHUNKS
    caches = cache_keys.shape[0]
    inner = w_query.shape[1]
    heads = inner // HD
    width = inner * n_head
    model = shard * n_head
    n_groups = n_seq // GROUP
    n_pairs = n_seq // 2
    old = caches * frame
    base = k32.shape[0]
    depth = kx.shape[1]
    link_rows = ss_send.shape[-1]
    member = seq % GROUP
    group = seq // GROUP
    x = seq % 2
    pair = seq // 2
    pair_in = member // 2
    mate_seq = pair * 2 + (1 - x)
    n_y = n_head // 2
    core = head % 2
    yy = head // 2
    mate = yy * 2 + (1 - core)
    sharp = HD ** (-0.5) * 1.4426950408889634

    barrier = pltpu.get_barrier_semaphore()
    for step in range(1, n_head):
        pl.semaphore_signal(
            barrier, inc=1, device_id={"head": lax.rem(head + step, n_head)},
            device_id_type=pl.DeviceIdType.MESH,
        )
    for step in range(1, n_seq):
        pl.semaphore_signal(
            barrier, inc=1, device_id={"seq": lax.rem(seq + step, n_seq)},
            device_id_type=pl.DeviceIdType.MESH,
        )
    x_in = [
        [
            pltpu.make_async_copy(
                source.at[:, :, pl.ds(c * HD, HD)], xg.at[kind, head, c], x_in_sem.at[kind, c]
            )
            for c in range(blocks)
        ]
        for kind, source in enumerate((x_noisy, x_clean))
    ]
    in_copies = [
        pltpu.make_async_copy(source, target, in_sem.at[i])
        for i, (source, target) in enumerate((
            (cache_keys, keys_vmem), (cache_values, values_vmem), (modulation, mod_vmem),
        ))
    ]
    w_copies = [
        pltpu.make_async_copy(w, w_vmem.at[i], w_sem.at[i])
        for i, w in enumerate((w_query, w_key, w_value))
    ]
    for copy in x_in[0] + in_copies[:2] + x_in[1] + in_copies[2:]:
        copy.start()
    for copy in x_in[0]:
        copy.wait()
    with span("p_barrier"):
        pl.semaphore_wait(barrier, n_head - 1 + n_seq - 1)

    def remote(src, dst, send, recv, axis, index):
        return pltpu.make_async_remote_copy(
            src_ref=src, dst_ref=dst, send_sem=send, recv_sem=recv,
            device_id={axis: index}, device_id_type=pl.DeviceIdType.MESH,
        )

    def x_copy(kind, slot, k, send, to):
        part = xg.at[kind, slot, pl.ds(k * chunk, chunk)]
        return remote(part, part, send, x_recv_sem.at[kind, slot, k], "head", to)

    x_sends = []

    def send_x(kind):
        for k in range(CHUNKS):
            for step in range(1, n_y):
                to = lax.rem(yy + step, n_y) * 2 + core
                x_sends.append(x_copy(kind, head, k, x_send_sem.at[kind, step, k], to))
                x_sends[-1].start()

    def send_mate(kind):
        for k in range(CHUNKS):
            x_sends.append(x_copy(kind, head, k, x_send_sem.at[kind, 0, k], mate))
            x_sends[-1].start()

    send_x(0)
    send_mate(0)

    half = HD // 2
    time_pairs = (HD - 4 * (HD // 6)) // 2
    freq = frequency[0:1, :]

    def lanes_of(count):
        lane = lax.broadcasted_iota(jnp.int32, (count, HD), 1)
        return (lane % half) < time_pairs, jnp.where(lane < half, -1.0, 1.0).astype(F32)

    with span("p_cachewait"):
        in_copies[0].wait()
        in_copies[1].wait()
        for copy in x_in[1]:
            copy.wait()
    send_x(1)
    for copy in w_copies:
        copy.start()

    is_time, sign = lanes_of(frame)
    space = (lax.broadcasted_iota(jnp.int32, (frame, HD), 0) + seq * frame).astype(F32)
    space_angle = space * freq
    space_cos = jnp.cos(space_angle)
    space_sin = jnp.sin(space_angle) * sign
    time_row = lax.broadcasted_iota(jnp.int32, (16, HD), 0)
    times = jnp.zeros((16, HD), F32)
    for f in range(caches):
        times = jnp.where(time_row == f, frame_pos[f].astype(F32), times)
    time_angle = times * freq
    time_cos = jnp.cos(time_angle)
    time_sin = jnp.sin(time_angle) * sign[0:1, :]

    def rotate(values, cos, sin):
        return values * cos + pltpu.roll(values, half, 1) * sin

    with span("p_rot"):
        spare = base - old
        v32[...] = jnp.zeros_like(v32)
        for f in range(caches):
            cos = jnp.where(is_time, time_cos[f : f + 1, :], space_cos)
            sin = jnp.where(is_time, time_sin[f : f + 1, :], space_sin)
            for h in range(heads):
                cols = slice(h * HD, (h + 1) * HD)
                at = slice(f * frame, (f + 1) * frame)
                turned = rotate(keys_vmem[f, :, cols].astype(F32), cos, sin)
                k32[at, cols] = turned
                if spare and f == caches - 1:
                    k32[old:base, cols] = turned[frame - spare :, :]
                v32[at, cols] = values_vmem[f, :, cols].astype(F32)
        for h in range(heads):
            cols = slice(h * HD, (h + 1) * HD)
            kst[h, :base, :] = k32[:, cols].astype(BF16)
            vst[h, :base, :] = v32[:, cols].astype(BF16)
            vst[h, base:, :] = jnp.zeros((depth - base, HD), BF16)

    bounds = ((0, base), (base, depth - base))

    def kv_pair(part, src, k_dst, v_dst, send, recv, to):
        begin, size = bounds[part]
        at = pl.ds(begin, size)
        return (
            remote(
                kst.at[src, at], k_dst.at[at], send.at[part, 0], recv.at[part, 0], "seq", to,
            ),
            remote(
                vst.at[src, at], v_dst.at[at, pl.ds(0, HD)], send.at[part, 1], recv.at[part, 1],
                "seq", to,
            ),
        )

    def kv_to(part, step):
        other = lax.rem(member + step, GROUP)
        return kv_pair(
            part, other, kx.at[member], vx.at[member], kv_send_sem.at[step],
            kv_recv_sem.at[member], group * GROUP + other,
        )

    def kv_from(part, step):
        other = lax.rem(member + step, GROUP)
        return kv_pair(
            part, other, kx.at[other], vx.at[other], kv_send_sem.at[step],
            kv_recv_sem.at[other], group * GROUP + other,
        )

    def shared_to(part):
        return kv_pair(part, GROUP, ks.at[x], vs.at[x], sh_send_sem, sh_recv_sem, mate_seq)

    def shared_from(part):
        return kv_pair(part, GROUP, ks.at[1 - x], vs.at[1 - x], sh_send_sem, sh_recv_sem, mate_seq)

    kv_sends = []

    def send_kv(part):
        copies = []
        for step in range(1, GROUP):
            copies += kv_to(part, step)
        copies += shared_to(part)
        for copy in copies:
            copy.start()
        kv_sends.extend(copies)
        begin, size = bounds[part]
        at = slice(begin, begin + size)
        kx[member, at, :] = kst[member, at, :]
        vx[member, at, :HD] = vst[member, at, :]
        ks[x, at, :] = kst[GROUP, at, :]
        vs[x, at, :HD] = vst[GROUP, at, :]

    with span("p_sendkv"):
        send_kv(0)

    place = lax.broadcasted_iota(jnp.int32, (depth, HD), 0)
    valid = (place < old) | ((place >= base) & (place < base + rows))
    ones = jnp.where(valid, 1.0, 0.0).astype(BF16)
    for i in range(GROUP):
        vx[i, :, HD:] = ones
    for i in range(2):
        vs[i, :, HD:] = ones

    is_time, sign = lanes_of(rows)
    row = lax.broadcasted_iota(jnp.int32, (rows, HD), 0)
    times = jnp.zeros((rows, HD), F32)
    for g in range(groups):
        times = jnp.where(row % groups == g, frame_pos[caches + g].astype(F32), times)
    space = (row // groups + seq * frame).astype(F32)
    angle = jnp.where(is_time, times, space) * freq
    table[0] = jnp.cos(angle)
    table[1] = jnp.sin(angle) * sign

    x_flat = xg.reshape(2 * n_head * blocks * rows, HD)

    def x_block(kind, slot, c):
        begin = ((kind * n_head + slot) * blocks + c) * rows
        if not isinstance(begin, int):
            begin = pl.multiple_of(begin, 8)
        return x_flat[pl.ds(begin, rows), :].astype(F32)

    def block_stats(kind, slot):
        total = x_block(kind, slot, 0)
        for c in range(1, blocks):
            total = total + x_block(kind, slot, c)
        total = jnp.sum(total, axis=-1, keepdims=True)
        centre = total / shard
        spread = jnp.zeros((rows, HD), F32)
        for c in range(blocks):
            away = x_block(kind, slot, c) - centre
            spread = spread + away * away
        return centre, jnp.sum(spread, axis=-1, keepdims=True)

    def gather_x(kind):
        forwards, stats = [], [block_stats(kind, head)]
        for step in range(1, n_y):
            source = lax.rem(yy + n_y - step, n_y) * 2 + core
            for k in range(CHUNKS):
                x_copy(kind, source, k, x_send_sem.at[kind, 0, k], mate).wait_recv()
                forwards.append(x_copy(kind, source, k, x_fwd_sem.at[kind, step, k], mate))
                forwards[-1].start()
            if step < n_y - 1:
                stats.append(block_stats(kind, source))
        if kind == 0:
            send_mate(1)
        for k in range(CHUNKS):
            x_copy(kind, mate, k, x_send_sem.at[kind, 0, k], mate).wait_recv()
        stats.append(block_stats(kind, mate))
        if n_y > 1:
            stats.append(block_stats(kind, lax.rem(yy + 1, n_y) * 2 + core))
        for step in range(1, n_y):
            source = lax.rem(yy + n_y - step, n_y) * 2 + (1 - core)
            for k in range(CHUNKS):
                x_copy(kind, source, k, x_send_sem.at[kind, 0, k], mate).wait_recv()
            stats.append(block_stats(kind, source))
        centre = stats[0][0]
        for other, _ in stats[1:]:
            centre = centre + other
        centre = centre / n_head
        spread = jnp.zeros((rows, 1), F32)
        for other, own in stats:
            spread = spread + own + shard * ((other - centre) * (other - centre))
        return forwards, centre, lax.rsqrt(spread / model + epsilon)

    def modulate(kind, step_index, j, centre, inverse):
        for c in range(blocks):
            columns = slice(j * shard + c * HD, j * shard + (c + 1) * HD)
            shift = mod_vmem[0, 0:1, columns]
            scale = mod_vmem[0, 1:2, columns]
            if step_index is not None:
                for i in range(1, mod_vmem.shape[0]):
                    shift = jnp.where(step_index == i, mod_vmem[i, 0:1, columns], shift)
                    scale = jnp.where(step_index == i, mod_vmem[i, 1:2, columns], scale)
            normed = (x_block(kind, j, c) - centre) * inverse
            y[kind, j, :, c * HD : (c + 1) * HD] = (normed * (1.0 + scale) + shift).astype(BF16)

    def project(kind, which, target):
        target[...] = jnp.zeros_like(target)

        @pl.loop(0, n_head)
        def _(j):
            begin = pl.multiple_of(j * shard, shard)
            target[...] += jnp.dot(
                y[kind, j], w_vmem[which, pl.ds(begin, shard), :], preferred_element_type=F32
            )

    def to_link(stats):
        tall = jnp.concatenate([stats, jnp.zeros((link_rows - rows, HD), F32)], axis=0)
        return tall.T[:8, :]

    def from_link(flat):
        tall = jnp.concatenate([flat, jnp.zeros((HD - flat.shape[0], link_rows), F32)], axis=0)
        return tall.T[:rows, :]

    def share_squares(kind, values):
        squares = jnp.sum(values * values, axis=-1, keepdims=True)
        flat = to_link(jnp.broadcast_to(squares, (rows, HD)))
        ss_send[kind] = flat
        copies = []
        for step in range(1, n_head):
            to = lax.rem(head + step, n_head)
            copies.append(
                remote(
                    ss_send.at[kind], ss_recv.at[kind, head], ss_send_sem.at[kind, step],
                    ss_recv_sem.at[kind, head], "head", to,
                )
            )
            copies[-1].start()
        return copies, flat

    def total_squares(kind, squares):
        for step in range(1, n_head):
            source = lax.rem(head + step, n_head)
            remote(
                ss_send.at[kind], ss_recv.at[kind, source], ss_send_sem.at[kind, step],
                ss_recv_sem.at[kind, source], "head", source,
            ).wait_recv()
            squares = squares + ss_recv[kind, source]
        return from_link(lax.rsqrt(squares / width + epsilon))[:, 0:1]

    in_copies[2].wait()
    with span("p_gx0"):
        forwards, centre, inverse = gather_x(0)
    with span("p_modproj"):
        for j in range(n_head):
            modulate(0, controls[0], j, centre, inverse)
        w_copies[0].wait()
        project(0, 0, acc)
    ss_copies, squares = share_squares(0, acc[...])
    with span("p_projk"):
        w_copies[1].wait()
        project(0, 1, acc_b)
    more, key_squares = share_squares(1, acc_b[...])
    ss_copies += more
    with span("p_totq"):
        inverse = total_squares(0, squares)
    with span("p_sendq"):
        for h in range(heads):
            cols = slice(h * HD, (h + 1) * HD)
            normed = acc[:, cols] * inverse * q_gain[cols][None, :]
            q_st[h] = rotate(normed, table[0], table[1]).astype(BF16)
        q_sends = []
        for g in list(range(1, n_groups)) + [0]:
            for step in range(GROUP):
                if g == 0 and step == 0:
                    continue
                other = lax.rem(member + step, GROUP)
                to = lax.rem(group + g, n_groups) * GROUP + other
                q_sends.append(
                    remote(
                        q_st.at[other], qx.at[seq], qx_send_sem.at[g * GROUP + step],
                        qx_recv_sem.at[seq], "seq", to,
                    )
                )
                q_sends[-1].start()
                if step % 2 == 0:
                    q_sends.append(
                        remote(
                            q_st.at[GROUP], qs.at[seq], qs_send_sem.at[g * GROUP + step],
                            qs_recv_sem.at[seq], "seq", to,
                        )
                    )
                    q_sends[-1].start()
        qx[seq] = q_st[member]
        qs[seq] = q_st[GROUP]

    with span("p_projv"):
        w_copies[2].wait()
        project(0, 2, acc)
    with span("p_newkv"):
        inverse = total_squares(1, key_squares)
        for h in range(heads):
            cols = slice(h * HD, (h + 1) * HD)
            normed = acc_b[:, cols] * inverse * k_gain[cols][None, :]
            fresh = rotate(normed, table[0], table[1]).astype(BF16)
            kst[h, base : base + rows, :] = fresh
            kst[h, base + rows :, :] = fresh[: depth - base - rows, :]
            vst[h, base : base + rows, :] = acc[:, cols].astype(BF16)
        send_kv(1)

    with span("p_gx1"):
        more, centre, inverse = gather_x(1)
        forwards += more
    with span("p_mod1"):
        for j in range(n_head):
            modulate(1, None, j, centre, inverse)
    with span("p_projck"):
        project(1, 1, acc_b)
    more, clean_squares = share_squares(2, acc_b[...])
    ss_copies += more

    with span("p_waitkv"):
        for part in range(2):
            for step in range(1, GROUP):
                for copy in kv_from(part, step):
                    copy.wait_recv()
            for copy in shared_from(part):
                copy.wait_recv()

    def q_from(source):
        return remote(
            q_st.at[0], qx.at[source], qx_send_sem.at[0], qx_recv_sem.at[source], "seq", mate_seq
        )

    def qs_from(source):
        return remote(
            q_st.at[0], qs.at[source], qs_send_sem.at[0], qs_recv_sem.at[source], "seq", mate_seq
        )

    def part_to(b):
        return (
            remote(
                part_x.at[b], px.at[seq], px_send_sem.at[b], px_recv_sem.at[seq], "seq", b,
            ),
            remote(
                stat_st.at[b], st.at[seq], st_send_sem.at[b], st_recv_sem.at[seq], "seq", b,
            ),
        )

    def part_from(b):
        return (
            remote(part_x.at[b], px.at[b], px_send_sem.at[b], px_recv_sem.at[b], "seq", b),
            remote(stat_st.at[b], st.at[b], st_send_sem.at[b], st_recv_sem.at[b], "seq", b),
        )

    def column_to(p):
        return remote(
            part_s.at[p], ps.at[pair], ps_send_sem.at[p], ps_recv_sem.at[pair], "seq", p * 2 + x,
        )

    def column_from(p):
        return remote(
            part_s.at[p], ps.at[p], ps_send_sem.at[p], ps_recv_sem.at[p], "seq", p * 2 + x,
        )

    def softmax(queries, keys, values):
        scores = lax.dot_general(
            queries, keys, (((1,), (1,)), ((), ())), preferred_element_type=F32
        )
        top = jnp.max(scores, axis=-1, keepdims=True)
        weights = jnp.exp2((scores - top) * sharp).astype(BF16)
        return top, jnp.dot(weights, values, preferred_element_type=F32)

    wide = lax.broadcasted_iota(jnp.int32, (rows, HD), 1)

    def other_pair(k):
        return lax.rem(group + k // 2, n_groups) * 2 + lax.rem(pair_in + k, 2)

    @pl.loop(0, n_pairs)
    def _(k):
        p = other_pair(k)
        with span("p_waitq"):
            @pl.when(k > 0)
            def _():
                for i in range(2):
                    q_from(p * 2 + i).wait_recv()
                qs_from(p * 2 + x).wait_recv()

            @pl.when(k == 0)
            def _():
                q_from(mate_seq).wait_recv()

        with span("p_attend"):
            top, sums = softmax(
                qx[pl.ds(p * 2, 2)].reshape(2 * rows, HD),
                kx[...].reshape(GROUP * depth, HD),
                vx[...].reshape(GROUP * depth, 2 * HD),
            )
            top_s, sums_s = softmax(
                qs[p * 2 + x], ks[...].reshape(2 * depth, HD), vs[...].reshape(2 * depth, 2 * HD)
            )
            part_s[p] = sums_s[:, :HD].astype(BF16)
            for i in range(2):
                at = slice(i * rows, (i + 1) * rows)
                part_x[p * 2 + i] = sums[at, :HD].astype(BF16)
                stats = jnp.where(wide == 0, top[at, :], sums[at, HD:])
                stats = jnp.where(wide == 2, top_s, stats)
                stats = jnp.where(wide == 3, sums_s[:, HD:], stats)
                stat_st[p * 2 + i] = to_link(stats)

        with span("p_sendpart"):
            @pl.when(k > 0)
            def _():
                for i in range(2):
                    for copy in part_to(p * 2 + i):
                        copy.start()
                column_to(p).start()

            @pl.when(k == 0)
            def _():
                for copy in part_to(mate_seq):
                    copy.start()

    px[seq] = part_x[seq]
    st[seq] = stat_st[seq]
    ps[pair] = part_s[pair]

    with span("p_projcv"):
        project(1, 2, acc)
        inverse = total_squares(2, clean_squares)
        for h in range(heads):
            cols = slice(h * HD, (h + 1) * HD)
            flip[0, h] = acc_b[:, cols] * inverse * k_gain[cols][None, :]
            flip[1, h] = acc[:, cols]
        for g in range(groups):
            at = pl.ds(g, frame, stride=groups)
            for h in range(heads):
                cols = slice(h * HD, (h + 1) * HD)
                fresh_keys[g, :, cols] = flip[0, h, at, :].astype(BF16)
                fresh_values[g, :, cols] = flip[1, h, at, :].astype(BF16)

    with span("p_waitpart"):
        @pl.loop(1, n_seq)
        def _(c):
            for copy in part_from(lax.rem(seq + c, n_seq)):
                copy.wait_recv()

        @pl.loop(1, n_pairs)
        def _(c):
            column_from(lax.rem(pair + c, n_pairs)).wait_recv()

    with span("p_final"):
        sources = [[(g * GROUP + h, px, g * GROUP + h, 0) for g in range(n_groups)] for h in range(GROUP)]
        sources.append([(p * 2 + x, ps, p, 2) for p in range(n_pairs)])
        lines = []
        for terms in sources:
            tops = [st[s, r : r + 1, :] for s, _, _, r in terms]
            top = functools.reduce(jnp.maximum, tops)
            shares = [jnp.exp2((t - top) * sharp) for t in tops]
            total = shares[0] * st[terms[0][0], terms[0][3] + 1 : terms[0][3] + 2, :]
            for share, (s, _, _, r) in zip(shares[1:], terms[1:]):
                total = total + share * st[s, r + 1 : r + 2, :]
            lines += [share / total for share in shares]
        lines.append(jnp.zeros((HD - len(lines), link_rows), F32))
        scales = jnp.concatenate(lines, axis=0).T[:rows, :]
        out_flat = out_ref.reshape(heads * rows, HD)
        at = 0
        for h, terms in enumerate(sources):
            result = jnp.zeros((rows, HD), F32)
            for _, source, slot, _ in terms:
                result = result + source[slot].astype(F32) * scales[:, at : at + 1]
                at += 1
            out_flat[h * rows : (h + 1) * rows, :] = result.astype(BF16)

    for copy in x_sends + forwards + ss_copies + kv_sends + q_sends:
        copy.wait_send()

    @pl.loop(1, n_seq)
    def _(c):
        for copy in part_to(lax.rem(seq + c, n_seq)):
            copy.wait_send()

    @pl.loop(1, n_pairs)
    def _(c):
        column_to(lax.rem(pair + c, n_pairs)).wait_send()


def write_kernel(
    controls, attended, keys, values, fresh_keys, fresh_values, out, new_keys, new_values, sem
):
    copies = [
        pltpu.make_async_copy(attended.at[h], out.at[:, :, pl.ds(h * HD, HD)], sem.at[h])
        for h in range(attended.shape[0])
    ]
    for copy in copies:
        copy.start()
    caches, groups = keys.shape[0], fresh_keys.shape[0]
    rolling = caches - controls[2]
    targets = [controls[2] + lax.rem(controls[1] + g, rolling) for g in range(groups)]
    for old, fresh, new in ((keys, fresh_keys, new_keys), (values, fresh_values, new_values)):
        for f in range(caches):
            kept = old[f]
            for g in range(groups):
                kept = jnp.where(targets[g] == f, fresh[g], kept)
            new[f] = kept
    for copy in copies:
        copy.wait()


def body(n_seq, n_head, hidden, clean, w_query, w_key, w_value, q_gain, k_gain, keys, values,
         modulation, controls, frame_pos):
    groups, frame, shard = hidden.shape
    caches = keys.shape[0]
    inner = w_query.shape[1]
    heads = inner // HD
    rows = groups * frame
    blocks = shard // HD
    base = -(-(caches * frame) // 16) * 16
    depth = -(-(base + rows) // 128) * 128
    half = HD // 2
    time_pairs = (HD - 4 * (HD // 6)) // 2
    pair = np.arange(half)
    exponent = np.where(pair < time_pairs, pair / time_pairs, (pair - time_pairs) / (half - time_pairs))
    line = np.power(10000.0, -exponent).astype(np.float32)
    frequency = jnp.asarray(np.tile(np.concatenate([line, line])[None, :], (8, 1)))
    vmem = pl.BlockSpec(memory_space=pltpu.VMEM)
    smem = pl.BlockSpec(memory_space=pltpu.SMEM)
    hbm = pl.BlockSpec(memory_space=pl.ANY)
    dma = pltpu.SemaphoreType.DMA
    n_pairs = n_seq // 2
    link_rows = -(-rows // 128) * 128
    fresh = jax.ShapeDtypeStruct((groups, frame, inner), BF16)
    attended = jax.ShapeDtypeStruct((heads, frame, groups, HD), BF16)
    attended, fresh_keys, fresh_values = pl.pallas_call(
        functools.partial(kernel, n_seq, n_head),
        out_shape=(attended, fresh, fresh),
        in_specs=[hbm, hbm, hbm, hbm, hbm, vmem, vmem, hbm, hbm, hbm, vmem, smem, smem],
        out_specs=(vmem, vmem, vmem),
        scratch_shapes=[
            pltpu.VMEM((3,) + w_query.shape, BF16),
            pltpu.VMEM(modulation.shape, F32),
            pltpu.VMEM(keys.shape, BF16),
            pltpu.VMEM(values.shape, BF16),
            pltpu.VMEM((2, n_head, blocks, frame, groups, HD), BF16),
            pltpu.VMEM((2, n_head, rows, shard), BF16),
            pltpu.VMEM((rows, inner), F32),
            pltpu.VMEM((rows, inner), F32),
            pltpu.VMEM((2, heads, rows, HD), F32),
            pltpu.VMEM((2, rows, HD), F32),
            pltpu.VMEM((base, inner), F32),
            pltpu.VMEM((base, inner), F32),
            pltpu.VMEM((heads, depth, HD), BF16),
            pltpu.VMEM((heads, depth, HD), BF16),
            pltpu.VMEM((GROUP, depth, HD), BF16),
            pltpu.VMEM((GROUP, depth, 2 * HD), BF16),
            pltpu.VMEM((2, depth, HD), BF16),
            pltpu.VMEM((2, depth, 2 * HD), BF16),
            pltpu.VMEM((heads, rows, HD), BF16),
            pltpu.VMEM((n_seq, rows, HD), BF16),
            pltpu.VMEM((n_seq, rows, HD), BF16),
            pltpu.VMEM((n_seq, rows, HD), BF16),
            pltpu.VMEM((n_pairs, rows, HD), BF16),
            pltpu.VMEM((n_seq, 8, link_rows), F32),
            pltpu.VMEM((n_seq, rows, HD), BF16),
            pltpu.VMEM((n_pairs, rows, HD), BF16),
            pltpu.VMEM((n_seq, 8, link_rows), F32),
            pltpu.VMEM((3, 8, link_rows), F32),
            pltpu.VMEM((3, n_head, 8, link_rows), F32),
            dma((3,)),
            dma((3,)),
            dma((2, blocks)),
            dma((2, n_head, CHUNKS)),
            dma((2, n_head, CHUNKS)),
            dma((2, n_head, CHUNKS)),
            dma((3, n_head)),
            dma((3, n_head)),
            dma((GROUP, 2, 2)),
            dma((GROUP, 2, 2)),
            dma((2, 2)),
            dma((2, 2)),
            dma((n_seq,)),
            dma((n_seq,)),
            dma((n_seq,)),
            dma((n_seq,)),
            dma((n_seq,)),
            dma((n_seq,)),
            dma((n_pairs,)),
            dma((n_pairs,)),
            dma((n_seq,)),
            dma((n_seq,)),
        ],
        compiler_params=pltpu.CompilerParams(
            collective_id=0, has_side_effects=True, vmem_limit_bytes=60 * 1024 * 1024
        ),
        name="block",
    )(jnp.transpose(hidden, (1, 0, 2)), jnp.transpose(clean, (1, 0, 2)), w_query, w_key, w_value,
      q_gain, k_gain, keys, values, modulation, frequency, controls, frame_pos)
    out, new_keys, new_values = pl.pallas_call(
        write_kernel,
        out_shape=(
            jax.ShapeDtypeStruct((frame, groups, inner), BF16),
            jax.ShapeDtypeStruct(keys.shape, BF16),
            jax.ShapeDtypeStruct(values.shape, BF16),
        ),
        in_specs=[smem, vmem, vmem, vmem, vmem, vmem],
        out_specs=(hbm, vmem, vmem),
        scratch_shapes=[dma((heads,))],
        name="write",
    )(controls, attended, keys, values, fresh_keys, fresh_values)
    return jnp.transpose(out, (1, 0, 2)), new_keys, new_values


def solution(mesh):
    split = P(None, "seq", "head")
    columns = P(None, "head")
    in_specs = (
        split, split, columns, columns, columns, P("head"), P("head"), split, split, P(), P(), P(),
    )
    step = functools.partial(body, mesh.shape["seq"], mesh.shape["head"])
    return jax.shard_map(
        step, mesh=mesh, in_specs=in_specs, out_specs=(split, split, split), check_vma=False
    )
```
